128 devices in a mesh: wide: 16 (over x, z_hi, core), narrow: 8 (over z_lo, y).
Axes of the slice: x: 4, y: 4, z: 4 (z_hi: 2, z_lo: 2; z = z_hi * 2 + z_lo), core: 2. Of those that a mesh axis runs over, the one named last changes fastest.
Arguments:
- activations: bfloat16 [2048, 16384], P('wide', 'narrow'), may hold values from -30 to 30, as said below
- weight_tile: bfloat16 [16384, 16384], P('wide', 'narrow'), may hold values from -3 to 3
- codes: int32 [16384, 16384], P('wide', 'narrow'), may hold values from -8 to 7
- group_scales: float32 [16384, 128], P('wide', 'narrow'), may hold values from 0.02 to 0.2
- right_factor: bfloat16 [16384, 256], replicated, may hold values from -0.046875 to 0.046875
Outputs:
- residual_product: float32 [16384, 256], P(('wide', 'narrow'))
- gram: float32 [256, 256], replicated
- hessian_tiles: bfloat16 [16384, 16384], P('wide', 'narrow')
The draws below stay inside these ranges and needn't reach their ends.
Inputs may be any that keep to these rules, and one draw needn't show every extreme that they name: `activations`: each token's features are a product of a token scale, a feature scale and a value.
All inputs are finite; a program needn't handle non-finite values.
Results may differ from the reference program's by a relative error of at most 0.0049.
Values may be sent and summed in bfloat16 or wider, within the bound.
A program may use at most 128 MiB of HBM per device.

```python
import math
import jax
import jax.numpy as jnp
from jax import lax

D = 16384
RANK = 256
GROUP = 128
TOKENS = 2048


def draw_activations(key, part):
    keys = jax.random.split(jax.random.fold_in(key, 71), 3)
    feature_scale = jnp.exp(jax.random.uniform(keys[0], (D,), jnp.float32, math.log(0.3), math.log(3.0)))
    token_scale = jnp.exp(jax.random.uniform(keys[1], (TOKENS,), jnp.float32, math.log(0.5), math.log(2.0)))
    base = jnp.clip(jax.random.normal(keys[2], (TOKENS, D), jnp.float32), -4.0, 4.0)
    return (base * token_scale[:, None] * feature_scale[None, :]).astype(jnp.bfloat16)


def plant(drawn, rng, least, largest):
    index_at = [jax.random.randint(jax.random.fold_in(rng, axis), (), 0, length) for axis, length in enumerate(drawn.shape)]
    longest = drawn.shape.index(max(drawn.shape))
    next_to = index_at[:longest] + [(index_at[longest] + 1) % drawn.shape[longest]] + index_at[longest + 1:]
    return drawn.at[tuple(index_at)].set(least).at[tuple(next_to)].set(largest)


def levels(stream_key, shape, pieces, smallest, largest):
    loudness = 1.0
    for dim, blocks in pieces:
        heights = jax.random.uniform(jax.random.fold_in(jax.random.fold_in(stream_key, 6), dim), (blocks,), jnp.float32, smallest / len(pieces), largest / len(pieces))
        loudness = loudness * jnp.repeat(jnp.exp(heights), shape[dim] // blocks).reshape((-1,) + (1,) * (len(shape) - 1 - dim))
    return loudness


def noise(stream_key, extent, width, reach, cuts=(), dtype=jnp.bfloat16):
    array = width * jax.random.normal(stream_key, extent, jnp.float32)
    if cuts:
        array = array * levels(stream_key, extent, cuts, -0.22, 0.18)
    return jnp.clip(array, -reach, reach).astype(dtype)


def setup_inputs(seed: int = 0) -> dict:
    seeds = jax.random.split(jax.random.key(seed), 6)
    activations = draw_activations(jax.random.fold_in(seeds[5], 71), 0)
    weight_tile = noise(seeds[1], (D, D), 0.5, 3.0, ((0, 16), (1, 8)))
    codes = plant(jax.random.randint(seeds[2], (D, D), -8, 8), jax.random.fold_in(seeds[2], 1), -8, 7).astype(jnp.int32)
    group_scales = jnp.clip(jnp.exp(math.log(0.2) - 2.3025851 * jax.random.uniform(seeds[3], (D, D // GROUP), jnp.float32) ** levels(seeds[3], (D, D // GROUP), ((0, 16), (1, 8)), -0.2, 0.2)), 0.02, 0.2)
    right_factor = noise(seeds[4], (D, RANK), D ** -0.5, 0.046875)
    return {"activations": activations, "weight_tile": weight_tile, "codes": codes, "group_scales": group_scales, "right_factor": right_factor}


def reference(activations, weight_tile, codes, group_scales, right_factor):
    hessian = lax.dot_general(activations, activations, (((0,), (0,)), ((), ())), preferred_element_type=jnp.float32) / TOKENS
    hessian_tiles = hessian.astype(jnp.bfloat16)
    groups = group_scales.shape[1]
    quantized = (codes.reshape(D, groups, GROUP).astype(jnp.float32) * group_scales[:, :, None]).reshape(D, D)
    residual = (weight_tile.astype(jnp.float32) - quantized).astype(jnp.bfloat16)
    hr_value = jnp.dot(hessian, right_factor.astype(jnp.float32), precision=lax.Precision.HIGHEST)
    hr_rounded = hr_value.astype(jnp.bfloat16)
    residual_product = jnp.dot(residual, hr_rounded, preferred_element_type=jnp.float32)
    gram = lax.dot_general(right_factor, hr_rounded, (((0,), (0,)), ((), ())), preferred_element_type=jnp.float32)
    return residual_product, gram, hessian_tiles
```

```python
import functools

import jax
import jax.numpy as jnp
from jax import lax
from jax.experimental import pallas as pl
from jax.experimental.pallas import tpu as pltpu
from jax.sharding import PartitionSpec as P

MESH = pl.DeviceIdType.MESH
F32 = jnp.float32
BF16 = jnp.bfloat16

TREES = {
    "A1": {"yp": [(0, 0), (1, 0), (2, 0), (1, 1), (2, 1), (3, 1)], "z": [(1, 0)]},
    "A2": {"yp": [(0, 0), (1, 0), (2, 0), (2, 1), (3, 1), (0, 1)], "z": [(2, 0)]},
    "B1": {"ym": [(0, 0), (3, 0), (2, 0), (3, 1), (2, 1), (1, 1)], "z": [(3, 0)]},
    "B2": {"ym": [(0, 0), (3, 0), (2, 0), (2, 1), (1, 1), (0, 1)], "z": [(2, 0)]},
    "Ca": {"z": [(0, 0), (1, 1), (2, 1), (3, 1)], "yp": [(0, 1), (1, 1)], "ym": [(0, 1)]},
    "Cb": {"z": [(0, 0), (1, 1), (2, 1), (3, 1)], "yp": [(0, 1)], "ym": [(0, 1), (3, 1)]},
}
DIRS = ("yp", "ym", "z")
LAG_OF_DEPTH = (0, 0, 1, 1, 2, 2, 2)

SLOTS = (
    (((0, 0, 0, 0), "A2"), ((0, 0, 0, 1), "B2"), ((0, 0, 1, 0), "Ca"), ((0, 0, 1, 1), "Cb")),
    (((3, 0, 0, 0), "A2"), ((1, 0, 0, 1), "B2"), ((0, 1, 0, 0), "Ca"),
     ((3, 0, 1, 0), "A2"), ((1, 0, 1, 1), "B2"), ((0, 1, 1, 0), "Cb")),
    (((3, 0, 0, 1), "A2"), ((1, 0, 0, 0), "B2"), ((0, 1, 0, 1), "Ca"),
     ((3, 0, 1, 1), "A1"), ((1, 0, 1, 0), "B1"), ((0, 1, 1, 1), "Cb")),
    (((2, 0, 0, 0), "A1"), ((2, 0, 0, 1), "B1"), ((2, 0, 1, 0), "A1"), ((2, 0, 1, 1), "B1")),
    (((3, 1, 0, 0), "A1"), ((1, 1, 0, 1), "B1"), ((3, 1, 1, 0), "A1"), ((1, 1, 1, 1), "B1")),
    (((3, 1, 0, 1), "A1"), ((1, 1, 0, 0), "B1"), ((3, 1, 1, 1), "A1"), ((1, 1, 1, 0), "B1")),
    (((2, 1, 0, 0), "A1"), ((2, 1, 0, 1), "B1"), ((2, 1, 1, 0), "Ca"), ((2, 1, 1, 1), "Cb")),
)
SUB = 32
HALF = 64
PIECE = 128


def step_from(role, direction):
    dy, dz = role
    if direction == "z":
        return (dy, 1 - dz)
    return ((dy + (1 if direction == "yp" else 3)) % 4, dz)


def depths(kind):
    depth = {(0, 0): 0}
    for _ in range(8):
        for direction, roles in TREES[kind].items():
            for role in roles:
                if role in depth:
                    target = step_from(role, direction)
                    if target not in depth:
                        depth[target] = depth[role] + 1
    return depth


def kernel(
    act, wt, codes, scales, rf,
    out_prod, out_gram, out_h,
    cols, rows, hacc, hout, res, cbuf, sbuf, rn,
    ypt, yrecv, yt, hrt, prod, prodrecv, gpart, grecv, gall,
    loc, csem, csend, rsem, rsend,
    yrs_r, yrs_s, yag_r, yag_s, ywd_r, ywd_s, prs_r, prs_s, grs_r, grs_s, gag_r, gag_s, osem,
):
    w = lax.axis_index("wide")
    n = lax.axis_index("narrow")
    c = w % 2
    zh = (w // 2) % 2
    x = w // 4
    zl = n // 4
    y = n % 4
    k = w // 2
    feats = cols.shape[2]
    half_feats = feats // 2
    rank = rf.shape[1]
    tokens = PIECE * 16

    def dev(x_, zh_, c_, zl_, y_):
        return (((x_ % 4) * 2 + zh_) * 2 + c_, zl_ * 4 + y_ % 4)

    partner = dev(x, zh, 1 - c, zl, y)
    right = dev(x + 1, zh, c, zl, y)
    left = dev(x + 3, zh, c, zl, y)
    across = dev(x, 1 - zh, c, zl, y)
    targets = {
        "yp": dev(x, zh, c, zl, y + 1),
        "ym": dev(x, zh, c, zl, y + 3),
        "z": dev(x, zh, c, 1 - zl, y),
    }

    def piece(dx, q, cc):
        return (((x + dx) % 4) * 2 + (1 - zh if q else zh)) * 2 + (1 - c if cc else c)

    own = cols.at[w]
    act_copy = pltpu.make_async_copy(act, own, loc.at[0])
    act_copy.start()
    rn_copy = pltpu.make_async_copy(rf.at[pl.ds(pl.multiple_of(n * feats, 128), feats)], rn, loc.at[1])
    rn_copy.start()
    s_copy = pltpu.make_async_copy(scales, sbuf, loc.at[2])
    s_copy.start()
    out_rows = res.shape[0]
    quarter = out_rows // 4
    wt_copies = []
    for i in range(4):
        sl = pl.ds(i * quarter, quarter)
        a = pltpu.make_async_copy(wt.at[sl], res.at[sl], loc.at[3 + i])
        b = pltpu.make_async_copy(codes.at[sl], cbuf.at[sl], loc.at[7 + i])
        a.start()
        b.start()
        wt_copies.append((a, b))

    barrier = pltpu.get_barrier_semaphore()
    for j in range(1, 8):
        pl.semaphore_signal(barrier, inc=1, device_id=(w, (n + j) % 8), device_id_type=MESH)
        pl.semaphore_signal(barrier, inc=1, device_id=(((k + j) % 8) * 2 + c, n), device_id_type=MESH)
    pl.semaphore_signal(barrier, inc=1, device_id=partner, device_id_type=MESH)
    act_copy.wait()
    pl.semaphore_wait(barrier, 15)

    def remote(src, dst, ssem, rsem_, to):
        cp = pltpu.make_async_remote_copy(src, dst, ssem, rsem_, device_id=to, device_id_type=MESH)
        cp.start()
        return cp

    def arrived(ref, sem):
        pltpu.make_async_copy(ref, ref, sem).wait()

    col_sends = []

    def col_part(p, sub):
        return cols.at[p, pl.ds(sub * SUB, SUB)]

    def col_send(p, sub, to):
        i = len(col_sends)
        ref = col_part(p, sub)
        remote(ref, ref, csend.at[i], csem.at[p, sub], to)
        col_sends.append(ref)

    def col_wait(p, sub):
        arrived(col_part(p, sub), csem.at[p, sub])

    for i in range(4):
        col_send(w, i, right)
        col_send(w, (i + 2) % 4, left)
        col_send(w, i, across)
        col_send(w, i, partner)

    def col_slot(s):
        mine = []
        if s == 0:
            pass
        elif s in (1, 4):
            q = int(s == 4)
            for i in range(2):
                mine.append((piece(3, q, 0), i, (right, partner)))
                mine.append((piece(1, q, 0), 2 + i, (left, partner)))
            if s == 1:
                for i in range(2):
                    mine.append((piece(0, 1, 0), i, (partner,)))
        elif s in (2, 5):
            q = int(s == 5)
            if s == 2:
                for i in range(2):
                    mine.append((piece(0, 1, 0), 2 + i, (partner,)))
            for i in range(2):
                mine.append((piece(3, q, 0), 2 + i, (partner,)))
                mine.append((piece(1, q, 0), i, (partner,)))
        elif s in (3, 6):
            q = int(s == 6)
            for i in range(4):
                mine.append((piece(2, q, 0), (0, 2, 1, 3)[i], (partner,)))
        for p, sub, to in mine:
            col_wait(p, sub)
            for t in to:
                col_send(p, sub, t)
        if s == 2:
            p = piece(0, 1, 0)
            for i in range(4):
                col_send(p, i, right)
                col_send(p, (i + 2) % 4, left)

    y_root = 2 * (x % 2) + zh
    zl_root = x // 2
    dy = (y + 4 - y_root) % 4
    dz = (zl + 2 - zl_root) % 2
    role = dz * 4 + dy
    is_root = role == 0

    def among(role_list):
        hit = role == role_list[0][1] * 4 + role_list[0][0]
        for a, b in role_list[1:]:
            hit = jnp.logical_or(hit, role == b * 4 + a)
        return hit

    passes = {kind: {d: among(r) for d, r in table.items()} for kind, table in TREES.items()}
    lag_is = {}
    for kind in TREES:
        by_lag = {}
        for r, d in depths(kind).items():
            by_lag.setdefault(LAG_OF_DEPTH[d], []).append(r)
        lag_is[kind] = {lag: among(r) for lag, r in by_lag.items()}

    def row_part(p, tok):
        return rows.at[p, pl.ds(tok, SUB)]

    def col_half_part(p, tok):
        return cols.at[p, pl.ds(tok, SUB), pl.ds(pl.multiple_of(c * half_feats, 128), half_feats)]

    def root_take(s):
        for (dx, q, cc, h), _ in SLOTS[s]:
            if cc:
                p = piece(dx, q, 1)
                col_wait(p, 2 * h)
                col_wait(p, 2 * h + 1)

        @pl.when(is_root)
        def _():
            for (dx, q, cc, h), _ in SLOTS[s]:
                p = piece(dx, q, cc)
                for i in range(2):
                    pltpu.make_async_copy(
                        col_half_part(p, h * HALF + i * SUB), row_part(p, h * HALF + i * SUB), rsem.at[p, 2 * h + i]
                    ).start()

    def row_slot(s):
        for lag in (2, 1, 0):
            m = s - lag
            if not 0 <= m < len(SLOTS):
                continue

            @pl.loop(0, 2)
            def _(i, m=m, lag=lag):
                for (dx, q, cc, h), kind in SLOTS[m]:
                    if lag not in lag_is[kind]:
                        continue

                    @pl.when(lag_is[kind][lag])
                    def _(dx=dx, q=q, cc=cc, h=h, kind=kind):
                        p = piece(dx, q, cc)
                        ref = row_part(p, pl.multiple_of(h * HALF + i * SUB, SUB))
                        sem = rsem.at[p, 2 * h + i]
                        arrived(ref, sem)
                        for d, hit in passes[kind].items():

                            @pl.when(hit)
                            def _(d=d):
                                remote(ref, ref, rsend.at[DIRS.index(d), p, h], sem, targets[d])

    def row_drain():
        for slot in SLOTS:
            for (dx, q, cc, h), kind in slot:
                for d, hit in passes[kind].items():

                    @pl.when(hit)
                    def _(dx=dx, q=q, cc=cc, h=h, d=d):
                        p = piece(dx, q, cc)
                        arrived(rows.at[p, pl.ds(h * HALF, HALF)], rsend.at[DIRS.index(d), p, h])

    blocks = 4
    block = hacc.shape[0] // blocks

    def hessian(dx, q, first=False, last=False):
        kk = ((x + dx) % 4) * 2 + (1 - zh if q else zh)

        @pl.loop(0, blocks)
        def _(b):
            off = pl.multiple_of(b * block, block)
            left_ = rows[pl.ds(2 * kk, 2), :, pl.ds(off, block)].reshape(2 * PIECE, block)
            right_ = cols[pl.ds(2 * kk, 2)].reshape(2 * PIECE, feats)
            part = lax.dot_general(left_, right_, (((0,), (0,)), ((), ())), preferred_element_type=F32)
            sl = pl.ds(off, block)
            if first:
                hacc[sl] = part
            elif last:
                hout[sl] = ((hacc[sl] + part) * (1.0 / tokens)).astype(BF16)
                pltpu.make_async_copy(hout.at[sl], out_h.at[sl], osem.at[b]).start()
            else:
                hacc[sl] += part

    def residual(i):
        a, b = wt_copies[i]
        a.wait()
        b.wait()
        step = 64

        @pl.loop(0, quarter // step)
        def _(j):
            sl = pl.ds(pl.multiple_of(i * quarter + j * step, step), step)
            for g in range(feats // 128):
                lanes = pl.ds(g * 128, 128)
                value = cbuf[sl, lanes].astype(F32) * sbuf[sl, g : g + 1]
                res[sl, lanes] = (res[sl, lanes].astype(F32) - value).astype(BF16)

    rn_copy.wait()
    ypt[...] = jnp.dot(cols[w], rn[...], preferred_element_type=F32).T
    share = rank // 8

    def narrow_block(ref, who):
        return ref.at[pl.ds(pl.multiple_of(who * share, share), share)]

    for j in range(1, 8):
        to = (n + j) % 8
        remote(narrow_block(ypt, to), yrecv.at[n], yrs_s.at[to], yrs_r.at[n], (w, to))
    yrecv[n] = ypt[pl.ds(pl.multiple_of(n * share, share), share)]

    root_take(0)
    row_slot(0)
    s_copy.wait()
    residual(0)

    for j in range(1, 8):
        who = (n + j) % 8
        arrived(yrecv.at[who], yrs_r.at[who])
    total = yrecv[0]
    for j in range(1, 8):
        total += yrecv[j]
    lanes_w = pl.ds(pl.multiple_of(w * PIECE, PIECE), PIECE)
    yt[pl.ds(pl.multiple_of(n * share, share), share), lanes_w] = total.astype(BF16)

    def y_block(who):
        return yt.at[pl.ds(pl.multiple_of(who * share, share), share), lanes_w]

    for j in range(1, 8):
        to = (n + j) % 8
        remote(y_block(n), y_block(n), yag_s.at[to], yag_r.at[n], (w, to))

    residual(1)
    col_slot(1)
    root_take(1)
    row_slot(1)

    for j in range(1, 8):
        who = (n + j) % 8
        arrived(y_block(who), yag_r.at[who])

    def y_piece(p):
        return yt.at[:, pl.ds(pl.multiple_of(p * PIECE, PIECE), PIECE)]

    for j in range(1, 8):
        to = (k + j) % 8
        remote(y_piece(w), y_piece(w), ywd_s.at[j], ywd_r.at[w], (2 * to + c, n))
    remote(y_piece(w), y_piece(w), ywd_s.at[0], ywd_r.at[w], partner)

    residual(2)
    col_slot(2)
    root_take(2)
    row_slot(2)
    hessian(0, 0, first=True)
    residual(3)
    col_slot(3)
    root_take(3)
    row_slot(3)
    for j in range(1, 8):
        p = ((k + j) % 8) * 2 + c
        arrived(y_piece(p), ywd_r.at[p])
        remote(y_piece(p), y_piece(p), ywd_s.at[7 + j], ywd_r.at[p], partner)
    col_slot(4)
    root_take(4)
    row_slot(4)
    hessian(3, 0)
    hessian(1, 0)
    col_slot(5)
    root_take(5)
    row_slot(5)
    hessian(0, 1)
    hessian(2, 0)
    for j in range(8):
        p = ((k + j) % 8) * 2 + 1 - c
        arrived(y_piece(p), ywd_r.at[p])
    col_slot(6)
    root_take(6)
    row_slot(6)

    hblock = 512

    @pl.loop(0, feats // hblock)
    def _(b):
        lanes = pl.ds(pl.multiple_of(b * hblock, hblock), hblock)
        value = jnp.dot(yt[...], cols[:, :, lanes].reshape(tokens, hblock), preferred_element_type=F32)
        hrt[:, lanes] = (value * (1.0 / tokens)).astype(BF16)

    row_slot(7)

    @pl.loop(0, 4)
    def _(b):
        sl = pl.ds(pl.multiple_of(b * quarter, quarter), quarter)
        prod[sl] = lax.dot_general(res[sl], hrt[...], (((1,), (1,)), ((), ())), preferred_element_type=F32)

    own_rows = out_rows // 8

    def prod_block(who):
        return prod.at[pl.ds(pl.multiple_of(who * own_rows, own_rows), own_rows)]

    for j in range(1, 8):
        to = (n + j) % 8
        remote(prod_block(to), prodrecv.at[n], prs_s.at[to], prs_r.at[n], (w, to))
    gpart[...] = jnp.dot(hrt[...], rn[...], preferred_element_type=F32)
    for j in range(1, 8):
        to = (n + j) % 8
        remote(narrow_block(gpart, to), grecv.at[n], grs_s.at[to], grs_r.at[n], (w, to))
    grecv[n] = gpart[pl.ds(pl.multiple_of(n * share, share), share)]
    prodrecv[n] = prod[pl.ds(pl.multiple_of(n * own_rows, own_rows), own_rows)]

    row_slot(8)
    hessian(3, 1)
    for j in range(1, 8):
        who = (n + j) % 8
        arrived(grecv.at[who], grs_r.at[who])
    gsum = grecv[0]
    for j in range(1, 8):
        gsum += grecv[j]
    gall[pl.ds(pl.multiple_of(n * share, share), share)] = gsum
    for j in range(1, 8):
        to = (n + j) % 8
        remote(narrow_block(gall, n), narrow_block(gall, n), gag_s.at[to], gag_r.at[n], (w, to))
    hessian(1, 1)
    hessian(2, 1, last=True)

    for j in range(1, 8):
        who = (n + j) % 8
        arrived(prodrecv.at[who], prs_r.at[who])
    psum = prodrecv[0]
    for j in range(1, 8):
        psum += prodrecv[j]
    out_prod[...] = psum
    for j in range(1, 8):
        who = (n + j) % 8
        arrived(narrow_block(gall, who), gag_r.at[who])
    out_gram[...] = gall[...].T

    for i, ref in enumerate(col_sends):
        arrived(ref, csend.at[i])
    row_drain()
    for j in range(1, 8):
        to = (n + j) % 8
        arrived(narrow_block(ypt, to), yrs_s.at[to])
        arrived(y_block(n), yag_s.at[to])
        arrived(prod_block(to), prs_s.at[to])
        arrived(narrow_block(gpart, to), grs_s.at[to])
        arrived(narrow_block(gall, n), gag_s.at[to])
    for j in range(15):
        arrived(y_piece(w), ywd_s.at[j])
    for b in range(blocks):
        sl = pl.ds(b * block, block)
        pltpu.make_async_copy(hout.at[sl], out_h.at[sl], osem.at[b]).wait()


def body(activations, weight_tile, codes, group_scales, right_factor):
    piece_tokens, feats = activations.shape
    out_rows = weight_tile.shape[0]
    rank = right_factor.shape[1]
    assert piece_tokens == PIECE
    dma = pltpu.SemaphoreType.DMA
    any_spec = pl.BlockSpec(memory_space=pl.ANY)
    vmem_spec = pl.BlockSpec(memory_space=pltpu.VMEM)
    return pl.pallas_call(
        kernel,
        out_shape=(
            jax.ShapeDtypeStruct((out_rows // 8, rank), F32),
            jax.ShapeDtypeStruct((rank, rank), F32),
            jax.ShapeDtypeStruct((out_rows, feats), BF16),
        ),
        in_specs=[any_spec] * 5,
        out_specs=(vmem_spec, vmem_spec, any_spec),
        scratch_shapes=[
            pltpu.VMEM((16, PIECE, feats), BF16),
            pltpu.VMEM((16, PIECE, feats // 2), BF16),
            pltpu.VMEM((out_rows, feats), F32),
            pltpu.VMEM((out_rows, feats), BF16),
            pltpu.VMEM((out_rows, feats), BF16),
            pltpu.VMEM((out_rows, feats), jnp.int32),
            pltpu.VMEM((out_rows, group_scales.shape[1]), F32),
            pltpu.VMEM((feats, rank), BF16),
            pltpu.VMEM((rank, PIECE), F32),
            pltpu.VMEM((8, rank // 8, PIECE), F32),
            pltpu.VMEM((rank, 16 * PIECE), BF16),
            pltpu.VMEM((rank, feats), BF16),
            pltpu.VMEM((out_rows, rank), F32),
            pltpu.VMEM((8, out_rows // 8, rank), F32),
            pltpu.VMEM((rank, rank), F32),
            pltpu.VMEM((8, rank // 8, rank), F32),
            pltpu.VMEM((rank, rank), F32),
            dma((11,)),
            dma((16, 4)),
            dma((64,)),
            dma((16, 4)),
            dma((3, 16, 2)),
            dma((8,)), dma((8,)), dma((8,)), dma((8,)), dma((16,)), dma((15,)),
            dma((8,)), dma((8,)), dma((8,)), dma((8,)), dma((8,)), dma((8,)),
            dma((4,)),
        ],
        compiler_params=pltpu.CompilerParams(
            collective_id=0, has_side_effects=True, vmem_limit_bytes=62 << 20
        ),
    )(activations, weight_tile, codes, group_scales, right_factor)


def solution(mesh):
    spec = P("wide", "narrow")
    return jax.shard_map(
        body,
        mesh=mesh,
        in_specs=(spec, spec, spec, spec, P()),
        out_specs=(P(("wide", "narrow"), None), P(), spec),
        check_vma=False,
    )
```

```python
import jax
import jax.numpy as jnp
from jax import lax
from jax.experimental import pallas as pl
from jax.experimental.pallas import tpu as pltpu
from jax.sharding import PartitionSpec as P

MESH = pl.DeviceIdType.MESH
F32 = jnp.float32
BF16 = jnp.bfloat16
DIRS = ("yp", "ym", "z")
SUB = 32
PIECE = 128

PLAN = (
    ("c", 0, 0, 0),
    ("c", 0, 0, 1),
    ("c", 0, 0, 2),
    ("c", 0, 0, 3),
    ("ydot",),
    ("r", 768, 0, 0, 0, 0, 0, 0, 0),
    ("r", 784, 0, 0, 0, 0, 0, 0, 0),
    ("r", 672, 0, 0, 0, 0, 0, 0, 0),
    ("r", 688, 0, 0, 0, 0, 0, 0, 0),
    ("o", 0, 0, 0),
    ("o", 0, 0, 1),
    ("res", 0),
    ("o", 0, 0, 2),
    ("r", 584, 0, 0, 0, 0, 0, 0, 0),
    ("o", 0, 0, 3),
    ("r", 792, 0, 0, 0, 0, 0, 0, 0),
    ("res", 1),
    ("r", 680, 0, 0, 0, 0, 0, 0, 0),
    ("r", 824, 0, 0, 0, 0, 0, 0, 0),
    ("c", 3, 0, 0),
    ("c", 1, 0, 2),
    ("res", 2),
    ("r", 643, 0, 0, 672, 0, 0, 0, 0),
    ("r", 609, 0, 0, 0, 0, 0, 0, 0),
    ("c", 0, 1, 0),
    ("res", 3),
    ("o", 3, 0, 0),
    ("o", 1, 0, 2),
    ("r", 644, 840, 0, 944, 0, 0, 0, 0),
    ("r", 651, 0, 0, 0, 0, 0, 0, 0),
    ("o", 0, 1, 0),
    ("r", 681, 0, 0, 0, 0, 0, 0, 0),
    ("c", 3, 0, 1),
    ("c", 1, 0, 3),
    ("r", 588, 0, 928, 680, 0, 0, 0, 0),
    ("r", 787, 0, 0, 0, 0, 0, 0, 0),
    ("r", 625, 0, 0, 0, 0, 0, 0, 0),
    ("c", 0, 1, 1),
    ("r", 788, 609, 0, 0, 0, 0, 0, 0),
    ("o", 3, 0, 1),
    ("o", 1, 0, 3),
    ("r", 667, 0, 584, 899, 0, 0, 0, 0),
    ("r", 633, 0, 0, 0, 0, 0, 0, 0),
    ("o", 0, 1, 1),
    ("r", 668, 0, 688, 0, 0, 0, 0, 0),
    ("c", 3, 0, 2),
    ("c", 1, 0, 0),
    ("r", 803, 544, 865, 900, 0, 0, 0, 0),
    ("r", 769, 844, 0, 0, 0, 0, 0, 0),
    ("c", 0, 1, 2),
    ("r", 612, 0, 936, 0, 0, 0, 0, 0),
    ("o", 3, 0, 2),
    ("o", 1, 0, 0),
    ("r", 619, 881, 0, 520, 0, 0, 0, 0),
    ("r", 585, 0, 0, 651, 0, 0, 0, 0),
    ("o", 0, 1, 2),
    ("r", 684, 560, 643, 0, 0, 0, 0, 0),
    ("c", 3, 0, 3),
    ("c", 1, 0, 1),
    ("r", 627, 889, 588, 545, 0, 0, 0, 0),
    ("r", 657, 552, 0, 937, 0, 0, 0, 0),
    ("c", 0, 1, 3),
    ("Q",),
    ("r", 628, 0, 644, 0, 0, 0, 0, 0),
    ("yred",),
    ("o", 3, 0, 3),
    ("r", 0, 0, 625, 0, 0, 0, 0, 0),
    ("o", 1, 0, 1),
    ("r", 699, 868, 0, 923, 704, 0, 0, 0),
    ("o", 0, 1, 3),
    ("r", 601, 515, 907, 524, 0, 584, 672, 688),
    ("r", 636, 619, 0, 0, 0, 0, 0, 0),
    ("c", 2, 0, 0),
    ("c", 2, 0, 2),
    ("r", 578, 516, 633, 924, 720, 588, 609, 643),
    ("r", 802, 841, 681, 561, 728, 672, 688, 644),
    ("r", 0, 0, 612, 940, 0, 625, 584, 0),
    ("r", 0, 0, 0, 0, 0, 0, 680, 0),
    ("c", 2, 0, 1),
    ("c", 2, 0, 3),
    ("r", 658, 523, 667, 569, 760, 633, 643, 609),
    ("r", 818, 883, 875, 913, 0, 0, 588, 681),
    ("r", 0, 628, 668, 0, 0, 0, 651, 0),
    ("r", 0, 553, 0, 0, 0, 0, 0, 0),
    ("o", 2, 0, 0),
    ("r", 650, 0, 0, 0, 0, 0, 0, 0),
    ("o", 2, 0, 2),
    ("r", 810, 0, 0, 0, 0, 0, 0, 0),
    ("o", 2, 0, 1),
    ("r", 794, 0, 0, 548, 0, 0, 0, 0),
    ("o", 2, 0, 3),
    ("r", 698, 0, 585, 955, 672, 688, 644, 584),
    ("r", 0, 0, 0, 0, 723, 612, 625, 0),
    ("c", 3, 1, 0),
    ("c", 1, 1, 2),
    ("r", 583, 539, 684, 555, 609, 832, 619, 667),
    ("r", 805, 857, 627, 914, 0, 680, 681, 768),
    ("r", 0, 0, 0, 0, 0, 0, 0, 588),
    ("o", 3, 1, 0),
    ("r", 0, 0, 0, 0, 724, 0, 633, 0),
    ("o", 1, 1, 2),
    ("r", 655, 540, 657, 521, 520, 585, 0, 668),
    ("r", 685, 0, 884, 0, 0, 784, 0, 912),
    ("r", 0, 0, 0, 0, 0, 643, 0, 0),
    ("yag",),
    ("r", 0, 892, 0, 906, 560, 0, 667, 625),
    ("r", 0, 0, 0, 0, 739, 0, 0, 0),
    ("c", 3, 1, 1),
    ("c", 1, 1, 3),
    ("r", 599, 556, 699, 512, 680, 627, 612, 684),
    ("r", 693, 512, 601, 563, 524, 856, 668, 792),
    ("r", 0, 578, 658, 954, 705, 651, 768, 619),
    ("r", 0, 528, 636, 528, 0, 601, 628, 657),
    ("r", 0, 529, 0, 564, 0, 824, 0, 952),
    ("r", 0, 839, 0, 911, 0, 644, 0, 633),
    ("c", 3, 1, 2),
    ("c", 1, 1, 0),
    ("r", 615, 571, 650, 537, 515, 851, 784, 699),
    ("r", 581, 599, 834, 685, 738, 681, 585, 544),
    ("r", 0, 530, 512, 0, 0, 636, 627, 612),
    ("r", 0, 0, 698, 0, 0, 0, 684, 0),
    ("o", 3, 1, 1),
    ("r", 799, 0, 0, 0, 561, 545, 0, 658),
    ("r", 0, 0, 0, 0, 754, 0, 0, 787),
    ("r", 0, 0, 0, 0, 651, 0, 0, 0),
    ("o", 1, 1, 3),
    ("r", 637, 0, 583, 572, 0, 667, 0, 0),
    ("o", 3, 1, 2),
    ("r", 623, 0, 0, 0, 0, 0, 0, 0),
    ("o", 1, 1, 0),
    ("r", 589, 536, 0, 693, 0, 0, 0, 628),
    ("c", 3, 1, 3),
    ("c", 1, 1, 1),
    ("r", 695, 615, 528, 536, 619, 788, 792, 916),
    ("r", 789, 522, 655, 514, 746, 583, 657, 0),
    ("r", 0, 0, 855, 0, 0, 0, 578, 0),
    ("ya",),
    ("r", 0, 568, 941, 568, 516, 668, 601, 585),
    ("r", 0, 570, 0, 519, 569, 867, 824, 650),
    ("r", 0, 837, 0, 0, 730, 0, 0, 803),
    ("o", 3, 1, 3),
    ("r", 0, 0, 0, 0, 0, 684, 0, 0),
    ("o", 1, 1, 1),
    ("r", 0, 531, 0, 0, 553, 0, 0, 627),
    ("c", 2, 1, 0),
    ("c", 2, 1, 2),
    ("r", 703, 637, 949, 695, 548, 769, 699, 698),
    ("r", 582, 527, 536, 531, 741, 657, 787, 552),
    ("r", 806, 0, 871, 535, 539, 0, 599, 578),
    ("r", 669, 0, 0, 0, 0, 0, 0, 0),
    ("yn", 3, 0),
    ("r", 0, 532, 0, 0, 0, 0, 636, 0),
    ("yn", 1, 0),
    ("r", 0, 879, 568, 532, 628, 866, 658, 897),
    ("r", 0, 557, 531, 547, 540, 699, 685, 655),
    ("r", 0, 547, 0, 959, 521, 882, 583, 601),
    ("r", 0, 565, 0, 551, 735, 0, 693, 802),
    ("r", 0, 845, 0, 0, 556, 0, 788, 599),
    ("c", 2, 1, 1),
    ("c", 2, 1, 3),
    ("o", 2, 1, 0),
    ("r", 654, 513, 0, 0, 0, 0, 0, 0),
    ("o", 2, 1, 2),
    ("r", 662, 838, 581, 513, 563, 658, 803, 636),
    ("r", 630, 0, 0, 925, 725, 555, 650, 523),
    ("r", 814, 0, 0, 0, 529, 581, 615, 0),
    ("o", 2, 1, 1),
    ("r", 0, 546, 0, 0, 0, 0, 0, 0),
    ("yn", 3, 1),
    ("yn", 1, 1),
    ("r", 0, 0, 0, 0, 0, 0, 0, 818),
    ("o", 2, 1, 3),
    ("r", 798, 0, 951, 546, 578, 810, 802, 0),
    ("r", 702, 0, 532, 0, 742, 0, 698, 0),
    ("yf", 0),
    ("r", 0, 562, 893, 662, 571, 693, 818, 583),
    ("r", 0, 630, 0, 0, 537, 623, 769, 938),
    ("r", 0, 0, 0, 0, 750, 858, 0, 0),
    ("r", 0, 0, 0, 0, 0, 685, 0, 0),
    ("yf", 1),
    ("r", 0, 0, 547, 517, 530, 589, 0, 703),
    ("r", 0, 0, 703, 0, 0, 650, 0, 0),
    ("r", 0, 0, 623, 0, 0, 0, 0, 0),
    ("yoth",),
    ("r", 0, 567, 669, 654, 0, 869, 695, 669),
    ("r", 0, 0, 0, 562, 0, 0, 581, 615),
    ("r", 0, 0, 0, 0, 0, 0, 655, 0),
    ("hr", 0),
    ("r", 0, 554, 546, 573, 734, 582, 0, 794),
    ("r", 0, 0, 589, 0, 599, 0, 0, 0),
    ("r", 0, 0, 0, 0, 572, 0, 0, 0),
    ("r", 0, 0, 0, 0, 693, 0, 0, 0),
    ("hr", 1),
    ("r", 0, 538, 918, 554, 0, 698, 637, 805),
    ("r", 0, 0, 562, 958, 0, 564, 623, 0),
    ("r", 0, 0, 0, 0, 0, 0, 810, 0),
    ("hr", 2),
    ("r", 0, 0, 582, 559, 519, 0, 0, 581),
    ("hr", 3),
    ("r", 0, 549, 513, 538, 522, 799, 794, 927),
    ("r", 0, 541, 886, 0, 0, 655, 703, 0),
    ("r", 0, 575, 910, 0, 0, 0, 0, 0),
    ("prod", 1),
    ("r", 0, 0, 554, 525, 615, 695, 669, 789),
    ("r", 0, 0, 0, 0, 685, 853, 589, 0),
    ("prod", 0),
    ("r", 0, 534, 702, 549, 570, 0, 662, 702),
    ("r", 0, 543, 0, 518, 517, 0, 805, 623),
    ("r", 0, 0, 0, 0, 0, 0, 0, 637),
    ("r", 0, 0, 0, 0, 0, 0, 0, 806),
    ("prod", 2),
    ("r", 0, 0, 538, 543, 0, 870, 799, 0),
    ("r", 0, 0, 0, 0, 0, 514, 630, 0),
    ("r", 0, 0, 0, 0, 0, 669, 0, 0),
    ("prod", 3),
    ("r", 0, 533, 0, 566, 527, 0, 582, 942),
    ("r", 0, 526, 0, 533, 559, 0, 0, 589),
    ("gram",),
    ("r", 0, 0, 549, 0, 695, 814, 702, 0),
    ("r", 0, 0, 0, 0, 0, 703, 654, 0),
    ("r", 0, 0, 0, 0, 0, 0, 789, 0),
    ("H", 0, 0, 0, 1, 0, 1),
    ("r", 0, 574, 0, 550, 637, 662, 806, 926),
    ("r", 0, 550, 0, 0, 0, 0, 0, 0),
    ("H", 0, 0, 0, 1, 1, 1),
    ("r", 0, 0, 543, 558, 541, 798, 814, 565),
    ("r", 0, 0, 0, 0, 525, 0, 0, 582),
    ("H", 1, 0, 3, 0, 0, 0),
    ("r", 0, 558, 533, 542, 0, 535, 0, 630),
    ("r", 0, 0, 0, 0, 0, 702, 0, 557),
    ("prodsend", 4),
    ("prodsend", 3),
    ("r", 0, 0, 0, 0, 0, 0, 798, 0),
    ("prodsend", 5),
    ("r", 0, 0, 0, 0, 0, 551, 0, 0),
    ("H", 1, 0, 3, 0, 1, 0),
    ("r", 0, 542, 550, 0, 518, 654, 0, 567),
    ("r", 0, 0, 0, 0, 662, 0, 0, 0),
    ("prodsend", 7),
    ("r", 0, 0, 0, 0, 575, 0, 0, 0),
    ("prodsend", 2),
    ("prodsend", 6),
    ("prodsend", 1),
    ("r", 0, 0, 558, 0, 0, 573, 0, 0),
    ("H", 2, 0, 1, 1, 0, 0),
    ("r", 0, 0, 0, 0, 630, 0, 0, 0),
    ("H", 2, 0, 1, 1, 1, 0),
    ("gramred",),
    ("r", 0, 0, 542, 0, 654, 566, 0, 534),
    ("r", 0, 0, 0, 0, 574, 0, 0, 526),
    ("H", 3, 1, 2, 1, 0, -1),
    ("H", 3, 1, 2, 1, 1, -1),
)

def kernel(
    act, wt, codes, scales, rf,
    out_prod, out_gram, out_h,
    cols, rows, hacc, res, cbuf, sbuf, scol, rn,
    ypt, yrecv, yt, hrt, prod, prodrecv, gpart, grecv, gall,
    loc, csem, csend, rsem, rsend,
    yrs_r, yrs_s, yag_r, yag_s, ywd_r, ywd_s, prs_r, prs_s, grs_r, grs_s, gag_r, gag_s,
):
    w = lax.axis_index("wide")
    n = lax.axis_index("narrow")
    c = lax.rem(w, 2)
    k = lax.div(w, 2)
    zh = lax.rem(k, 2)
    x = lax.div(k, 2)
    zl = lax.div(n, 4)
    y = lax.rem(n, 4)
    feats = cols.shape[2]
    half_feats = feats // 2
    rank = rf.shape[1]
    tokens = PIECE * 16

    def dev(x_, zh_, c_, zl_, y_):
        return ((lax.rem(x_, 4) * 2 + zh_) * 2 + c_, zl_ * 4 + lax.rem(y_, 4))

    partner = dev(x, zh, 1 - c, zl, y)
    right = dev(x + 1, zh, c, zl, y)
    left = dev(x + 3, zh, c, zl, y)
    across = dev(x, 1 - zh, c, zl, y)
    targets = {
        "yp": dev(x, zh, c, zl, y + 1),
        "ym": dev(x, zh, c, zl, y + 3),
        "z": dev(x, zh, c, 1 - zl, y),
    }

    def peer(j):
        return lax.rem(n + j, 8)

    def piece(dx, q, cc):
        return (lax.rem(x + dx, 4) * 2 + lax.rem(zh + q, 2)) * 2 + lax.rem(c + cc, 2)

    act_copy = pltpu.make_async_copy(act, cols.at[w], loc.at[0])
    act_copy.start()
    rn_copy = pltpu.make_async_copy(rf.at[pl.ds(pl.multiple_of(n * feats, 128), feats)], rn, loc.at[1])
    rn_copy.start()
    s_copy = pltpu.make_async_copy(scales, sbuf, loc.at[2])
    s_copy.start()
    out_rows = res.shape[0]
    quarter = out_rows // 4
    wt_copies = []
    for i in range(4):
        sl = pl.ds(i * quarter, quarter)
        a = pltpu.make_async_copy(wt.at[sl], res.at[sl], loc.at[3 + i])
        b = pltpu.make_async_copy(codes.at[sl], cbuf.at[sl], loc.at[7 + i])
        a.start()
        b.start()
        wt_copies.append((a, b))

    barrier = pltpu.get_barrier_semaphore()
    for j in range(1, 8):
        pl.semaphore_signal(barrier, inc=1, device_id=(w, peer(j)), device_id_type=MESH)
        pl.semaphore_signal(barrier, inc=1, device_id=(lax.rem(k + j, 8) * 2 + c, n), device_id_type=MESH)
    pl.semaphore_signal(barrier, inc=1, device_id=partner, device_id_type=MESH)
    act_copy.wait()
    pl.semaphore_wait(barrier, 15)

    def remote(src, dst, ssem, rsem_, to):
        pltpu.make_async_remote_copy(src, dst, ssem, rsem_, device_id=to, device_id_type=MESH).start()

    def arrived(ref, sem):
        pltpu.make_async_copy(ref, ref, sem).wait()

    col_sends = []

    def col_part(p, sub):
        return cols.at[p, pl.ds(sub * SUB, SUB)]

    def col_send(p, sub, to):
        ref = col_part(p, sub)
        remote(ref, ref, csend.at[0], csem.at[p, sub], to)
        col_sends.append(ref)

    for i in range(4):
        col_send(w, i, right)
        col_send(w, (i + 2) % 4, left)
        col_send(w, i, across)
        col_send(w, i, partner)

    dy = lax.rem(y + 4 - (2 * lax.rem(x, 2) + zh), 4)
    dz = lax.rem(zl + 2 - lax.div(x, 2), 2)
    role = dz * 4 + dy
    is_role = [role == r for r in range(8)]
    role_one = [jnp.where(hit, 1, 0) for hit in is_role]

    def root_take(p, sub):
        @pl.when(is_role[0])
        def _():
            src = cols.at[p, pl.ds(sub * SUB, SUB), pl.ds(pl.multiple_of(c * half_feats, 128), half_feats)]
            pltpu.make_async_copy(src, rows.at[p, pl.ds(sub * SUB, SUB)], rsem.at[p, sub]).start()

    def row_step(entries):
        code = sum(entry * one for entry, one in zip(entries, role_one, strict=True) if entry)

        @pl.when(code >= 512)
        def _():
            p = piece(lax.rem(code, 4), lax.rem(lax.div(code, 4), 2), lax.rem(lax.div(code, 8), 2))
            sub = lax.rem(lax.div(code, 16), 4)
            ref = rows.at[p, pl.ds(pl.multiple_of(sub * SUB, SUB), SUB)]
            arrived(ref, rsem.at[p, sub])
            for i, d in enumerate(DIRS):
                bit = 64 << i
                if any(entry & bit for entry in entries):

                    @pl.when(lax.rem(lax.div(code, bit), 2) == 1)
                    def _(i=i, d=d):
                        remote(ref, ref, rsend.at[i], rsem.at[p, sub], targets[d])

    def col_arrival(dx, q, sub):
        if (dx, q) != (0, 0):
            p = piece(dx, q, 0)
            arrived(col_part(p, sub), csem.at[p, sub])
            if dx == 3 and sub < 2:
                col_send(p, sub, right)
            if dx == 1 and sub >= 2:
                col_send(p, sub, left)
            col_send(p, sub, partner)
        root_take(piece(dx, q, 0), sub)

    def other_arrival(dx, q, sub):
        p = piece(dx, q, 1)
        arrived(col_part(p, sub), csem.at[p, sub])
        root_take(p, sub)

    def spread_across():
        p = piece(0, 1, 0)
        for i in range(4):
            col_send(p, i, right)
            col_send(p, (i + 2) % 4, left)

    block = hacc.shape[0] // 4

    def hessian(dx0, q0, dx1, q1, half, place):
        chips = [lax.rem(x + dx, 4) * 2 + lax.rem(zh + q, 2) for dx, q in ((dx0, q0), (dx1, q1))]

        @pl.loop(0, 2)
        def _(i):
            off = pl.multiple_of((2 * half + i) * block, block)
            sl = pl.ds(off, block)
            row_side = jnp.concatenate(
                [rows[pl.ds(2 * kk, 2), :, pl.ds(off, block)].reshape(2 * PIECE, block) for kk in chips], axis=0
            )
            col_side = jnp.concatenate([cols[pl.ds(2 * kk, 2)].reshape(2 * PIECE, feats) for kk in chips], axis=0)
            part = lax.dot_general(row_side, col_side, (((0,), (0,)), ((), ())), preferred_element_type=F32)
            if place > 0:
                hacc[sl] = part
            elif place < 0:
                out_h[sl] = ((hacc[sl] + part) * (1.0 / tokens)).astype(BF16)
            else:
                hacc[sl] += part

    def residual(i):
        if i == 0:
            s_copy.wait()
            scol[...] = sbuf[...].T
        a, b = wt_copies[i]
        a.wait()
        b.wait()
        step = 64

        @pl.loop(0, quarter // step)
        def _(j):
            sl = pl.ds(pl.multiple_of(i * quarter + j * step, step), step)
            for g in range(feats // 128):
                lanes = pl.ds(g * 128, 128)
                value = cbuf[sl, lanes].astype(F32) * scol[sl, g : g + 1]
                res[sl, lanes] = (res[sl, lanes].astype(F32) - value).astype(BF16)

    share = rank // 8

    def narrow_rows(who):
        return pl.ds(pl.multiple_of(who * share, share), share)

    def narrow_block(ref, who):
        return ref.at[narrow_rows(who)]

    def y_block(who):
        return yt.at[w, narrow_rows(who)]

    def y_piece(p):
        return yt.at[p]

    def sum_of(ref, sem):
        for j in range(1, 8):
            arrived(ref.at[peer(j)], sem.at[peer(j)])
        total = ref[0].astype(F32)
        for j in range(1, 8):
            total += ref[j].astype(F32)
        return total

    def y_dot():
        rn_copy.wait()
        ypt[...] = jnp.dot(cols[w], rn[...], preferred_element_type=F32).T
        for j in range(1, 8):
            to = peer(j)
            remote(narrow_block(ypt, to), yrecv.at[n], yrs_s.at[0], yrs_r.at[n], (w, to))
        yrecv[n] = ypt[narrow_rows(n)]

    def y_reduce():
        yt[w, narrow_rows(n)] = sum_of(yrecv, yrs_r).astype(BF16)
        for j in range(1, 8):
            remote(y_block(n), y_block(n), yag_s.at[0], yag_r.at[n], (w, peer(j)))

    def y_half(p, h):
        return yt.at[p, pl.ds(h * (rank // 2), rank // 2)]

    def y_send(p, to):
        remote(y_piece(p), y_piece(p), ywd_s.at[0], ywd_r.at[p, 0], to)

    def y_half_send(p, h, to):
        remote(y_half(p, h), y_half(p, h), ywd_s.at[0], ywd_r.at[p, h], to)

    def y_spread():
        for j in range(1, 8):
            arrived(y_block(peer(j)), yag_r.at[peer(j)])
        for to in (right, left, across, partner):
            y_send(w, to)

    def y_across():
        p = piece(0, 1, 0)
        arrived(y_piece(p), ywd_r.at[p, 0])
        for to in (right, left, partner):
            y_send(p, to)

    def y_beside(dx, q):
        p = piece(dx, q, 0)
        arrived(y_piece(p), ywd_r.at[p, 0])
        y_half_send(p, int(dx == 1), left if dx == 1 else right)
        y_send(p, partner)

    def y_opposite(q):
        p = piece(2, q, 0)
        for h in range(2):
            arrived(y_half(p, h), ywd_r.at[p, h])
        y_send(p, partner)

    def y_others():
        for dx in range(4):
            for q in range(2):
                p = piece(dx, q, 1)
                arrived(y_piece(p), ywd_r.at[p, 0])

    hblock = feats // 4

    def h_times_r(b):
        lanes = pl.ds(b * hblock, hblock)
        every = jnp.concatenate([yt[p] for p in range(16)], axis=1)
        value = jnp.dot(every, cols[:, :, lanes].reshape(tokens, hblock), preferred_element_type=F32)
        hrt[:, lanes] = (value * (1.0 / tokens)).astype(BF16)

    def product(b):
        sl = pl.ds(b * quarter, quarter)
        value = lax.dot_general(res[sl], hrt[...], (((1,), (1,)), ((), ())), preferred_element_type=F32)
        prod[sl] = value.astype(BF16)

    own_rows = out_rows // 8

    def prod_rows(who):
        return pl.ds(pl.multiple_of(who * own_rows, own_rows), own_rows)

    def product_send(j):
        to = peer(j)
        remote(prod.at[prod_rows(to)], prodrecv.at[n], prs_s.at[0], prs_r.at[n], (w, to))
        if j == 1:
            prodrecv[n] = prod[prod_rows(n)]

    gshare = rank // 16

    def gram_rows(ref, who):
        return ref.at[pl.ds(pl.multiple_of(who * gshare, gshare), gshare)]

    def gram_part():
        gpart[...] = jnp.dot(hrt[...], rn[...], preferred_element_type=F32)
        for j in range(1, 8):
            to = peer(j)
            remote(gram_rows(gpart, w), grecv.at[n], grs_s.at[0], grs_r.at[n], (w, to))
        grecv[n] = gpart[pl.ds(pl.multiple_of(w * gshare, gshare), gshare)]

    def gram_send(p, to):
        remote(gram_rows(gall, p), gram_rows(gall, p), gag_s.at[0], gag_r.at[p], to)

    def gram_reduce():
        gall[pl.ds(pl.multiple_of(w * gshare, gshare), gshare)] = sum_of(grecv, grs_r)
        for j in range(1, 8):
            gram_send(w, (lax.rem(k + j, 8) * 2 + c, n))
        gram_send(w, partner)

    steps = {
        "c": col_arrival, "o": other_arrival, "Q": spread_across, "H": hessian, "res": residual,
        "ydot": y_dot, "yred": y_reduce, "yag": y_spread, "ya": y_across, "yn": y_beside, "yf": y_opposite, "yoth": y_others,
        "hr": h_times_r, "prod": product, "prodsend": product_send, "gram": gram_part, "gramred": gram_reduce,
    }
    for name, *rest in PLAN:
        if name == "r":
            row_step(rest)
        else:
            steps[name](*rest)

    for j in range(1, 8):
        p = lax.rem(k + j, 8) * 2 + c
        arrived(gram_rows(gall, p), gag_r.at[p])
        gram_send(p, partner)
    out_prod[...] = sum_of(prodrecv, prs_r)
    for j in range(8):
        p = lax.rem(k + j, 8) * 2 + 1 - c
        arrived(gram_rows(gall, p), gag_r.at[p])
    out_gram[...] = gall[...].T

    arrived(hacc.at[pl.ds(0, len(col_sends) * 16)], csend.at[0])
    for r in range(8):

        @pl.when(is_role[r])
        def _(r=r):
            for i in range(3):
                sent = sum(1 for step in PLAN if step[0] == "r" and step[1 + r] & (64 << i))
                if sent:
                    arrived(hacc.at[pl.ds(0, sent * 8)], rsend.at[i])

    arrived(yrecv.at[pl.ds(0, 7)], yrs_s.at[0])
    arrived(ypt.at[pl.ds(0, 7 * share // 2)], yag_s.at[0])
    arrived(yt.at[pl.ds(0, 15)], ywd_s.at[0])
    arrived(prodrecv.at[pl.ds(0, 7)], prs_s.at[0])
    arrived(grecv.at[pl.ds(0, 7)], grs_s.at[0])
    arrived(gpart.at[pl.ds(0, 15 * gshare)], gag_s.at[0])


def store(prod, gram, hess, out_prod, out_gram, out_h, sem):
    copies = [
        pltpu.make_async_copy(src, dst, sem.at[i])
        for i, (src, dst) in enumerate(((hess, out_h), (prod, out_prod), (gram, out_gram)))
    ]
    for copy in copies:
        copy.start()
    for copy in copies:
        copy.wait()


def body(activations, weight_tile, codes, group_scales, right_factor):
    piece_tokens, feats = activations.shape
    out_rows = weight_tile.shape[0]
    rank = right_factor.shape[1]
    groups = group_scales.shape[1]
    assert piece_tokens == PIECE
    dma = pltpu.SemaphoreType.DMA
    any_spec = pl.BlockSpec(memory_space=pl.ANY)
    vmem_spec = pl.BlockSpec(memory_space=pltpu.VMEM)
    shapes = (((out_rows // 8, rank), F32), ((rank, rank), F32), ((out_rows, feats), BF16))
    parts = pl.pallas_call(
        kernel,
        out_shape=tuple(pltpu.VMEM(s, d) for s, d in shapes),
        in_specs=[any_spec] * 5,
        out_specs=(vmem_spec,) * 3,
        scratch_shapes=[
            pltpu.VMEM((16, PIECE, feats), BF16),
            pltpu.VMEM((16, PIECE, feats // 2), BF16),
            pltpu.VMEM((out_rows, feats), F32),
            pltpu.VMEM((out_rows, feats), BF16),
            pltpu.VMEM((out_rows, feats), jnp.int32),
            pltpu.VMEM((groups, out_rows), F32),
            pltpu.VMEM((out_rows, groups), F32),
            pltpu.VMEM((feats, rank), BF16),
            pltpu.VMEM((rank, PIECE), F32),
            pltpu.VMEM((8, rank // 8, PIECE), F32),
            pltpu.VMEM((16, rank, PIECE), BF16),
            pltpu.VMEM((rank, feats), BF16),
            pltpu.VMEM((out_rows, rank), BF16),
            pltpu.VMEM((8, out_rows // 8, rank), BF16),
            pltpu.VMEM((rank, rank), F32),
            pltpu.VMEM((8, rank // 16, rank), F32),
            pltpu.VMEM((rank, rank), F32),
            dma((11,)),
            dma((16, 4)),
            dma((1,)),
            dma((16, 4)),
            dma((3,)),
            dma((8,)), dma((1,)), dma((8,)), dma((1,)), dma((16, 2)), dma((1,)),
            dma((8,)), dma((1,)), dma((8,)), dma((1,)), dma((16,)), dma((1,)),
        ],
        compiler_params=pltpu.CompilerParams(
            collective_id=0, has_side_effects=True, vmem_limit_bytes=52 << 20
        ),
    )(activations, weight_tile, codes, group_scales.T, right_factor)
    return tuple(pl.pallas_call(
        store,
        out_shape=tuple(jax.ShapeDtypeStruct(s, d) for s, d in shapes),
        in_specs=[vmem_spec] * 3,
        out_specs=(any_spec,) * 3,
        scratch_shapes=[dma((3,))],
        compiler_params=pltpu.CompilerParams(vmem_limit_bytes=8 << 20),
    )(*parts))


def solution(mesh):
    spec = P("wide", "narrow")
    return jax.shard_map(
        body,
        mesh=mesh,
        in_specs=(spec, spec, spec, spec, P()),
        out_specs=(P(("wide", "narrow"), None), P(), spec),
        check_vma=False,
    )
```

```python
import jax
import jax.numpy as jnp
from jax import lax
from jax.experimental import pallas as pl
from jax.experimental.pallas import tpu as pltpu
from jax.sharding import PartitionSpec as P

MESH = pl.DeviceIdType.MESH
F32 = jnp.float32
BF16 = jnp.bfloat16
DIRS = ("yp", "ym", "z")
SUB = 32
PIECE = 128

PLAN = (
    ("c", 0, 0, 0),
    ("c", 0, 0, 1),
    ("c", 0, 0, 2),
    ("c", 0, 0, 3),
    ("ydot",),
    ("r", 768, 0, 0, 0, 0, 0, 0, 0),
    ("r", 784, 0, 0, 0, 0, 0, 0, 0),
    ("r", 672, 0, 0, 0, 0, 0, 0, 0),
    ("r", 688, 0, 0, 0, 0, 0, 0, 0),
    ("o", 0, 0, 0),
    ("o", 0, 0, 1),
    ("res", 0),
    ("o", 0, 0, 2),
    ("r", 584, 0, 0, 0, 0, 0, 0, 0),
    ("o", 0, 0, 3),
    ("r", 792, 0, 0, 0, 0, 0, 0, 0),
    ("res", 1),
    ("r", 680, 0, 0, 0, 0, 0, 0, 0),
    ("r", 824, 0, 0, 0, 0, 0, 0, 0),
    ("c", 3, 0, 0),
    ("c", 1, 0, 2),
    ("res", 2),
    ("r", 643, 0, 0, 672, 0, 0, 0, 0),
    ("r", 609, 0, 0, 0, 0, 0, 0, 0),
    ("c", 0, 1, 0),
    ("res", 3),
    ("o", 3, 0, 0),
    ("o", 1, 0, 2),
    ("r", 644, 840, 0, 944, 0, 0, 0, 0),
    ("r", 651, 0, 0, 0, 0, 0, 0, 0),
    ("o", 0, 1, 0),
    ("r", 681, 0, 0, 0, 0, 0, 0, 0),
    ("c", 3, 0, 1),
    ("c", 1, 0, 3),
    ("r", 588, 0, 928, 680, 0, 0, 0, 0),
    ("r", 787, 0, 0, 0, 0, 0, 0, 0),
    ("r", 625, 0, 0, 0, 0, 0, 0, 0),
    ("c", 0, 1, 1),
    ("r", 788, 609, 0, 0, 0, 0, 0, 0),
    ("o", 3, 0, 1),
    ("o", 1, 0, 3),
    ("r", 667, 0, 584, 899, 0, 0, 0, 0),
    ("r", 633, 0, 0, 0, 0, 0, 0, 0),
    ("o", 0, 1, 1),
    ("r", 668, 0, 688, 0, 0, 0, 0, 0),
    ("c", 3, 0, 2),
    ("c", 1, 0, 0),
    ("r", 803, 544, 865, 900, 0, 0, 0, 0),
    ("r", 769, 844, 0, 0, 0, 0, 0, 0),
    ("c", 0, 1, 2),
    ("r", 612, 0, 936, 0, 0, 0, 0, 0),
    ("o", 3, 0, 2),
    ("o", 1, 0, 0),
    ("r", 619, 881, 0, 520, 0, 0, 0, 0),
    ("r", 585, 0, 0, 651, 0, 0, 0, 0),
    ("o", 0, 1, 2),
    ("r", 684, 560, 643, 0, 0, 0, 0, 0),
    ("c", 3, 0, 3),
    ("c", 1, 0, 1),
    ("r", 627, 889, 588, 545, 0, 0, 0, 0),
    ("r", 657, 552, 0, 937, 0, 0, 0, 0),
    ("c", 0, 1, 3),
    ("Q",),
    ("r", 628, 0, 644, 0, 0, 0, 0, 0),
    ("yred",),
    ("o", 3, 0, 3),
    ("r", 0, 0, 625, 0, 0, 0, 0, 0),
    ("o", 1, 0, 1),
    ("r", 699, 868, 0, 923, 704, 0, 0, 0),
    ("o", 0, 1, 3),
    ("r", 601, 515, 907, 524, 0, 584, 672, 688),
    ("r", 636, 619, 0, 0, 0, 0, 0, 0),
    ("c", 2, 0, 0),
    ("c", 2, 0, 2),
    ("r", 578, 516, 633, 924, 720, 588, 609, 643),
    ("r", 802, 841, 681, 561, 728, 672, 688, 644),
    ("r", 0, 0, 612, 940, 0, 625, 584, 0),
    ("r", 0, 0, 0, 0, 0, 0, 680, 0),
    ("c", 2, 0, 1),
    ("c", 2, 0, 3),
    ("r", 658, 523, 667, 569, 760, 633, 643, 609),
    ("r", 818, 883, 875, 913, 0, 0, 588, 681),
    ("r", 0, 628, 668, 0, 0, 0, 651, 0),
    ("r", 0, 553, 0, 0, 0, 0, 0, 0),
    ("o", 2, 0, 0),
    ("r", 650, 0, 0, 0, 0, 0, 0, 0),
    ("o", 2, 0, 2),
    ("r", 810, 0, 0, 0, 0, 0, 0, 0),
    ("o", 2, 0, 1),
    ("r", 794, 0, 0, 548, 0, 0, 0, 0),
    ("o", 2, 0, 3),
    ("r", 698, 0, 585, 955, 672, 688, 644, 584),
    ("r", 0, 0, 0, 0, 723, 612, 625, 0),
    ("c", 3, 1, 0),
    ("c", 1, 1, 2),
    ("r", 583, 539, 684, 555, 609, 832, 619, 667),
    ("r", 805, 857, 627, 914, 0, 680, 681, 768),
    ("r", 0, 0, 0, 0, 0, 0, 0, 588),
    ("o", 3, 1, 0),
    ("r", 0, 0, 0, 0, 724, 0, 633, 0),
    ("o", 1, 1, 2),
    ("r", 655, 540, 657, 521, 520, 585, 0, 668),
    ("r", 685, 0, 884, 0, 0, 784, 0, 912),
    ("r", 0, 0, 0, 0, 0, 643, 0, 0),
    ("yag",),
    ("r", 0, 892, 0, 906, 560, 0, 667, 625),
    ("r", 0, 0, 0, 0, 739, 0, 0, 0),
    ("c", 3, 1, 1),
    ("c", 1, 1, 3),
    ("r", 599, 556, 699, 512, 680, 627, 612, 684),
    ("r", 693, 512, 601, 563, 524, 856, 668, 792),
    ("r", 0, 578, 658, 954, 705, 651, 768, 619),
    ("r", 0, 528, 636, 528, 0, 601, 628, 657),
    ("r", 0, 529, 0, 564, 0, 824, 0, 952),
    ("r", 0, 839, 0, 911, 0, 644, 0, 633),
    ("c", 3, 1, 2),
    ("c", 1, 1, 0),
    ("r", 615, 571, 650, 537, 515, 851, 784, 699),
    ("r", 581, 599, 834, 685, 738, 681, 585, 544),
    ("r", 0, 530, 512, 0, 0, 636, 627, 612),
    ("r", 0, 0, 698, 0, 0, 0, 684, 0),
    ("o", 3, 1, 1),
    ("r", 799, 0, 0, 0, 561, 545, 0, 658),
    ("r", 0, 0, 0, 0, 754, 0, 0, 787),
    ("r", 0, 0, 0, 0, 651, 0, 0, 0),
    ("o", 1, 1, 3),
    ("r", 637, 0, 583, 572, 0, 667, 0, 0),
    ("o", 3, 1, 2),
    ("r", 623, 0, 0, 0, 0, 0, 0, 0),
    ("o", 1, 1, 0),
    ("r", 589, 536, 0, 693, 0, 0, 0, 628),
    ("c", 3, 1, 3),
    ("c", 1, 1, 1),
    ("r", 695, 615, 528, 536, 619, 788, 792, 916),
    ("r", 789, 522, 655, 514, 746, 583, 657, 0),
    ("r", 0, 0, 855, 0, 0, 0, 578, 0),
    ("ya",),
    ("r", 0, 568, 941, 568, 516, 668, 601, 585),
    ("r", 0, 570, 0, 519, 569, 867, 824, 650),
    ("r", 0, 837, 0, 0, 730, 0, 0, 803),
    ("o", 3, 1, 3),
    ("r", 0, 0, 0, 0, 0, 684, 0, 0),
    ("o", 1, 1, 1),
    ("r", 0, 531, 0, 0, 553, 0, 0, 627),
    ("c", 2, 1, 0),
    ("c", 2, 1, 2),
    ("r", 703, 637, 949, 695, 548, 769, 699, 698),
    ("r", 582, 527, 536, 531, 741, 657, 787, 552),
    ("r", 806, 0, 871, 535, 539, 0, 599, 578),
    ("r", 669, 0, 0, 0, 0, 0, 0, 0),
    ("yn", 3, 0),
    ("r", 0, 532, 0, 0, 0, 0, 636, 0),
    ("yn", 1, 0),
    ("r", 0, 879, 568, 532, 628, 866, 658, 897),
    ("r", 0, 557, 531, 547, 540, 699, 685, 655),
    ("r", 0, 547, 0, 959, 521, 882, 583, 601),
    ("r", 0, 565, 0, 551, 735, 0, 693, 802),
    ("r", 0, 845, 0, 0, 556, 0, 788, 599),
    ("c", 2, 1, 1),
    ("c", 2, 1, 3),
    ("o", 2, 1, 0),
    ("r", 654, 513, 0, 0, 0, 0, 0, 0),
    ("o", 2, 1, 2),
    ("r", 662, 838, 581, 513, 563, 658, 803, 636),
    ("r", 630, 0, 0, 925, 725, 555, 650, 523),
    ("r", 814, 0, 0, 0, 529, 581, 615, 0),
    ("o", 2, 1, 1),
    ("r", 0, 546, 0, 0, 0, 0, 0, 0),
    ("yn", 3, 1),
    ("yn", 1, 1),
    ("r", 0, 0, 0, 0, 0, 0, 0, 818),
    ("o", 2, 1, 3),
    ("r", 798, 0, 951, 546, 578, 810, 802, 0),
    ("r", 702, 0, 532, 0, 742, 0, 698, 0),
    ("yf", 0),
    ("r", 0, 562, 893, 662, 571, 693, 818, 583),
    ("r", 0, 630, 0, 0, 537, 623, 769, 938),
    ("r", 0, 0, 0, 0, 750, 858, 0, 0),
    ("r", 0, 0, 0, 0, 0, 685, 0, 0),
    ("yf", 1),
    ("r", 0, 0, 547, 517, 530, 589, 0, 703),
    ("r", 0, 0, 703, 0, 0, 650, 0, 0),
    ("r", 0, 0, 623, 0, 0, 0, 0, 0),
    ("yoth",),
    ("r", 0, 567, 669, 654, 0, 869, 695, 669),
    ("r", 0, 0, 0, 562, 0, 0, 581, 615),
    ("r", 0, 0, 0, 0, 0, 0, 655, 0),
    ("hr", 0),
    ("r", 0, 554, 546, 573, 734, 582, 0, 794),
    ("r", 0, 0, 589, 0, 599, 0, 0, 0),
    ("r", 0, 0, 0, 0, 572, 0, 0, 0),
    ("r", 0, 0, 0, 0, 693, 0, 0, 0),
    ("hr", 1),
    ("r", 0, 538, 918, 554, 0, 698, 637, 805),
    ("r", 0, 0, 562, 958, 0, 564, 623, 0),
    ("r", 0, 0, 0, 0, 0, 0, 810, 0),
    ("hr", 2),
    ("r", 0, 0, 582, 559, 519, 0, 0, 581),
    ("hr", 3),
    ("r", 0, 549, 513, 538, 522, 799, 794, 927),
    ("r", 0, 541, 886, 0, 0, 655, 703, 0),
    ("r", 0, 575, 910, 0, 0, 0, 0, 0),
    ("r", 0, 0, 554, 525, 615, 695, 669, 789),
    ("r", 0, 0, 0, 0, 685, 853, 589, 0),
    ("prod", 0),
    ("r", 0, 534, 702, 549, 570, 0, 662, 702),
    ("r", 0, 543, 0, 518, 517, 0, 805, 623),
    ("r", 0, 0, 0, 0, 0, 0, 0, 637),
    ("r", 0, 0, 0, 0, 0, 0, 0, 806),
    ("r", 0, 0, 538, 543, 0, 870, 799, 0),
    ("r", 0, 0, 0, 0, 0, 514, 630, 0),
    ("r", 0, 0, 0, 0, 0, 669, 0, 0),
    ("prod", 1),
    ("r", 0, 533, 0, 566, 527, 0, 582, 942),
    ("r", 0, 526, 0, 533, 559, 0, 0, 589),
    ("gram",),
    ("r", 0, 0, 549, 0, 695, 814, 702, 0),
    ("r", 0, 0, 0, 0, 0, 703, 654, 0),
    ("r", 0, 0, 0, 0, 0, 0, 789, 0),
    ("H", 0, 0, 0, 1, 0, 1),
    ("r", 0, 574, 0, 550, 637, 662, 806, 926),
    ("r", 0, 550, 0, 0, 0, 0, 0, 0),
    ("H", 0, 0, 0, 1, 1, 1),
    ("r", 0, 0, 543, 558, 541, 798, 814, 565),
    ("r", 0, 0, 0, 0, 525, 0, 0, 582),
    ("H", 1, 0, 3, 0, 0, 0),
    ("r", 0, 558, 533, 542, 0, 535, 0, 630),
    ("r", 0, 0, 0, 0, 0, 702, 0, 557),
    ("prodsend", 4),
    ("prodsend", 3),
    ("r", 0, 0, 0, 0, 0, 0, 798, 0),
    ("prodsend", 5),
    ("r", 0, 0, 0, 0, 0, 551, 0, 0),
    ("H", 1, 0, 3, 0, 1, 0),
    ("r", 0, 542, 550, 0, 518, 654, 0, 567),
    ("r", 0, 0, 0, 0, 662, 0, 0, 0),
    ("prodsend", 7),
    ("r", 0, 0, 0, 0, 575, 0, 0, 0),
    ("prodsend", 2),
    ("prodsend", 6),
    ("prodsend", 1),
    ("r", 0, 0, 558, 0, 0, 573, 0, 0),
    ("H", 2, 0, 1, 1, 0, 0),
    ("r", 0, 0, 0, 0, 630, 0, 0, 0),
    ("H", 2, 0, 1, 1, 1, 0),
    ("gramred",),
    ("r", 0, 0, 542, 0, 654, 566, 0, 534),
    ("r", 0, 0, 0, 0, 574, 0, 0, 526),
    ("H", 3, 1, 2, 1, 0, -1),
    ("H", 3, 1, 2, 1, 1, -1),
)

def kernel(
    act, wt, codes, scales, rf,
    out_prod, out_gram, out_h,
    cols, rows, hacc, res, cbuf, sbuf, scol, rn,
    ypt, yrecv, yt, hrt, prod, prodrecv, gpart, grecv, gall,
    loc, csem, csend, rsem, rsend,
    yrs_r, yrs_s, yag_r, yag_s, ywd_r, ywd_s, prs_r, prs_s, grs_r, grs_s, gag_r, gag_s,
):
    w = lax.axis_index("wide")
    n = lax.axis_index("narrow")
    c = lax.rem(w, 2)
    k = lax.div(w, 2)
    zh = lax.rem(k, 2)
    x = lax.div(k, 2)
    zl = lax.div(n, 4)
    y = lax.rem(n, 4)
    feats = cols.shape[2]
    half_feats = feats // 2
    rank = rf.shape[1]
    tokens = PIECE * 16

    def dev(x_, zh_, c_, zl_, y_):
        return ((lax.rem(x_, 4) * 2 + zh_) * 2 + c_, zl_ * 4 + lax.rem(y_, 4))

    partner = dev(x, zh, 1 - c, zl, y)
    right = dev(x + 1, zh, c, zl, y)
    left = dev(x + 3, zh, c, zl, y)
    across = dev(x, 1 - zh, c, zl, y)
    targets = {
        "yp": dev(x, zh, c, zl, y + 1),
        "ym": dev(x, zh, c, zl, y + 3),
        "z": dev(x, zh, c, 1 - zl, y),
    }

    def peer(j):
        return lax.rem(n + j, 8)

    def piece(dx, q, cc):
        return (lax.rem(x + dx, 4) * 2 + lax.rem(zh + q, 2)) * 2 + lax.rem(c + cc, 2)

    act_copy = pltpu.make_async_copy(act, cols.at[w], loc.at[0])
    act_copy.start()
    rn_copy = pltpu.make_async_copy(rf.at[pl.ds(pl.multiple_of(n * feats, 128), feats)], rn, loc.at[1])
    rn_copy.start()
    s_copy = pltpu.make_async_copy(scales, sbuf, loc.at[2])
    s_copy.start()
    out_rows = res.shape[0]
    quarter = out_rows // 4
    wt_copies = []
    for i in range(4):
        sl = pl.ds(i * quarter, quarter)
        a = pltpu.make_async_copy(wt.at[sl], res.at[sl], loc.at[3 + i])
        b = pltpu.make_async_copy(codes.at[sl], cbuf.at[sl], loc.at[7 + i])
        a.start()
        b.start()
        wt_copies.append((a, b))

    barrier = pltpu.get_barrier_semaphore()
    for j in range(1, 8):
        pl.semaphore_signal(barrier, inc=1, device_id=(w, peer(j)), device_id_type=MESH)
        pl.semaphore_signal(barrier, inc=1, device_id=(lax.rem(k + j, 8) * 2 + c, n), device_id_type=MESH)
    pl.semaphore_signal(barrier, inc=1, device_id=partner, device_id_type=MESH)
    act_copy.wait()
    pl.semaphore_wait(barrier, 15)

    def remote(src, dst, ssem, rsem_, to):
        pltpu.make_async_remote_copy(src, dst, ssem, rsem_, device_id=to, device_id_type=MESH).start()

    def arrived(ref, sem):
        pltpu.make_async_copy(ref, ref, sem).wait()

    col_sends = []

    def col_part(p, sub):
        return cols.at[p, pl.ds(sub * SUB, SUB)]

    def col_send(p, sub, to):
        ref = col_part(p, sub)
        remote(ref, ref, csend.at[0], csem.at[p, sub], to)
        col_sends.append(ref)

    for i in range(4):
        col_send(w, i, right)
        col_send(w, (i + 2) % 4, left)
        col_send(w, i, across)
        col_send(w, i, partner)

    dy = lax.rem(y + 4 - (2 * lax.rem(x, 2) + zh), 4)
    dz = lax.rem(zl + 2 - lax.div(x, 2), 2)
    role = dz * 4 + dy
    is_role = [role == r for r in range(8)]
    role_one = [jnp.where(hit, 1, 0) for hit in is_role]

    def root_take(p, sub):
        @pl.when(is_role[0])
        def _():
            src = cols.at[p, pl.ds(sub * SUB, SUB), pl.ds(pl.multiple_of(c * half_feats, 128), half_feats)]
            pltpu.make_async_copy(src, rows.at[p, pl.ds(sub * SUB, SUB)], rsem.at[p, sub]).start()

    def row_step(entries):
        code = sum(entry * one for entry, one in zip(entries, role_one, strict=True) if entry)

        @pl.when(code >= 512)
        def _():
            p = piece(lax.rem(code, 4), lax.rem(lax.div(code, 4), 2), lax.rem(lax.div(code, 8), 2))
            sub = lax.rem(lax.div(code, 16), 4)
            ref = rows.at[p, pl.ds(pl.multiple_of(sub * SUB, SUB), SUB)]
            arrived(ref, rsem.at[p, sub])
            for i, d in enumerate(DIRS):
                bit = 64 << i
                if any(entry & bit for entry in entries):

                    @pl.when(lax.rem(lax.div(code, bit), 2) == 1)
                    def _(i=i, d=d):
                        remote(ref, ref, rsend.at[i], rsem.at[p, sub], targets[d])

    def col_arrival(dx, q, sub):
        if (dx, q) != (0, 0):
            p = piece(dx, q, 0)
            arrived(col_part(p, sub), csem.at[p, sub])
            if dx == 3 and sub < 2:
                col_send(p, sub, right)
            if dx == 1 and sub >= 2:
                col_send(p, sub, left)
            col_send(p, sub, partner)
        root_take(piece(dx, q, 0), sub)

    def other_arrival(dx, q, sub):
        p = piece(dx, q, 1)
        arrived(col_part(p, sub), csem.at[p, sub])
        root_take(p, sub)

    def spread_across():
        p = piece(0, 1, 0)
        for i in range(4):
            col_send(p, i, right)
            col_send(p, (i + 2) % 4, left)

    block = hacc.shape[0] // 4

    def hessian(dx0, q0, dx1, q1, half, place):
        chips = [lax.rem(x + dx, 4) * 2 + lax.rem(zh + q, 2) for dx, q in ((dx0, q0), (dx1, q1))]

        @pl.loop(0, 2)
        def _(i):
            off = pl.multiple_of((2 * half + i) * block, block)
            sl = pl.ds(off, block)
            row_side = jnp.concatenate(
                [rows[pl.ds(2 * kk, 2), :, pl.ds(off, block)].reshape(2 * PIECE, block) for kk in chips], axis=0
            )
            col_side = jnp.concatenate([cols[pl.ds(2 * kk, 2)].reshape(2 * PIECE, feats) for kk in chips], axis=0)
            part = lax.dot_general(row_side, col_side, (((0,), (0,)), ((), ())), preferred_element_type=F32)
            if place > 0:
                hacc[sl] = part
            elif place < 0:
                out_h[sl] = ((hacc[sl] + part) * (1.0 / tokens)).astype(BF16)
            else:
                hacc[sl] += part

    def residual(i):
        if i == 0:
            s_copy.wait()
            scol[...] = sbuf[...].T
        a, b = wt_copies[i]
        a.wait()
        b.wait()
        step = 64

        @pl.loop(0, quarter // step)
        def _(j):
            sl = pl.ds(pl.multiple_of(i * quarter + j * step, step), step)
            for g in range(feats // 128):
                lanes = pl.ds(g * 128, 128)
                value = cbuf[sl, lanes].astype(F32) * scol[sl, g : g + 1]
                res[sl, lanes] = (res[sl, lanes].astype(F32) - value).astype(BF16)

    share = rank // 8

    def narrow_rows(who):
        return pl.ds(pl.multiple_of(who * share, share), share)

    def narrow_block(ref, who):
        return ref.at[narrow_rows(who)]

    def y_block(who):
        return yt.at[w, narrow_rows(who)]

    def y_piece(p):
        return yt.at[p]

    def sum_of(ref, sem):
        for j in range(1, 8):
            arrived(ref.at[peer(j)], sem.at[peer(j)])
        total = ref[0].astype(F32)
        for j in range(1, 8):
            total += ref[j].astype(F32)
        return total

    def y_dot():
        rn_copy.wait()
        ypt[...] = jnp.dot(cols[w], rn[...], preferred_element_type=F32).T
        for j in range(1, 8):
            to = peer(j)
            remote(narrow_block(ypt, to), yrecv.at[n], yrs_s.at[0], yrs_r.at[n], (w, to))
        yrecv[n] = ypt[narrow_rows(n)]

    def y_reduce():
        yt[w, narrow_rows(n)] = sum_of(yrecv, yrs_r).astype(BF16)
        for j in range(1, 8):
            remote(y_block(n), y_block(n), yag_s.at[0], yag_r.at[n], (w, peer(j)))

    def y_half(p, h):
        return yt.at[p, pl.ds(h * (rank // 2), rank // 2)]

    def y_send(p, to):
        remote(y_piece(p), y_piece(p), ywd_s.at[0], ywd_r.at[p, 0], to)

    def y_half_send(p, h, to):
        remote(y_half(p, h), y_half(p, h), ywd_s.at[0], ywd_r.at[p, h], to)

    def y_spread():
        for j in range(1, 8):
            arrived(y_block(peer(j)), yag_r.at[peer(j)])
        for to in (right, left, across, partner):
            y_send(w, to)

    def y_across():
        p = piece(0, 1, 0)
        arrived(y_piece(p), ywd_r.at[p, 0])
        for to in (right, left, partner):
            y_send(p, to)

    def y_beside(dx, q):
        p = piece(dx, q, 0)
        arrived(y_piece(p), ywd_r.at[p, 0])
        y_half_send(p, int(dx == 1), left if dx == 1 else right)
        y_send(p, partner)

    def y_opposite(q):
        p = piece(2, q, 0)
        for h in range(2):
            arrived(y_half(p, h), ywd_r.at[p, h])
        y_send(p, partner)

    def y_others():
        for dx in range(4):
            for q in range(2):
                p = piece(dx, q, 1)
                arrived(y_piece(p), ywd_r.at[p, 0])

    hblock = feats // 4

    def h_times_r(b):
        lanes = pl.ds(b * hblock, hblock)
        every = jnp.concatenate([yt[p] for p in range(16)], axis=1)
        value = jnp.dot(every, cols[:, :, lanes].reshape(tokens, hblock), preferred_element_type=F32)
        hrt[:, lanes] = (value * (1.0 / tokens)).astype(BF16)

    def product(b):
        sl = pl.ds(b * (out_rows // 2), out_rows // 2)
        value = lax.dot_general(res[sl], hrt[...], (((1,), (1,)), ((), ())), preferred_element_type=F32)
        prod[sl] = value.astype(BF16)

    own_rows = out_rows // 8

    def prod_rows(who):
        return pl.ds(pl.multiple_of(who * own_rows, own_rows), own_rows)

    def product_send(j):
        to = peer(j)
        remote(prod.at[prod_rows(to)], prodrecv.at[n], prs_s.at[0], prs_r.at[n], (w, to))
        if j == 1:
            prodrecv[n] = prod[prod_rows(n)]

    gshare = rank // 16

    def gram_rows(ref, who):
        return ref.at[pl.ds(pl.multiple_of(who * gshare, gshare), gshare)]

    def gram_part():
        gpart[...] = jnp.dot(hrt[...], rn[...], preferred_element_type=F32)
        for j in range(1, 8):
            to = peer(j)
            remote(gram_rows(gpart, w), grecv.at[n], grs_s.at[0], grs_r.at[n], (w, to))
        grecv[n] = gpart[pl.ds(pl.multiple_of(w * gshare, gshare), gshare)]

    def gram_send(p, to):
        remote(gram_rows(gall, p), gram_rows(gall, p), gag_s.at[0], gag_r.at[p], to)

    def gram_reduce():
        gall[pl.ds(pl.multiple_of(w * gshare, gshare), gshare)] = sum_of(grecv, grs_r)
        for j in range(1, 8):
            gram_send(w, (lax.rem(k + j, 8) * 2 + c, n))
        gram_send(w, partner)

    steps = {
        "c": col_arrival, "o": other_arrival, "Q": spread_across, "H": hessian, "res": residual,
        "ydot": y_dot, "yred": y_reduce, "yag": y_spread, "ya": y_across, "yn": y_beside, "yf": y_opposite, "yoth": y_others,
        "hr": h_times_r, "prod": product, "prodsend": product_send, "gram": gram_part, "gramred": gram_reduce,
    }
    for name, *rest in PLAN:
        if name == "r":
            row_step(rest)
        else:
            steps[name](*rest)

    for j in range(1, 8):
        p = lax.rem(k + j, 8) * 2 + c
        arrived(gram_rows(gall, p), gag_r.at[p])
        gram_send(p, partner)
    out_prod[...] = sum_of(prodrecv, prs_r)
    for j in range(8):
        p = lax.rem(k + j, 8) * 2 + 1 - c
        arrived(gram_rows(gall, p), gag_r.at[p])
    out_gram[...] = gall[...].T

    arrived(hacc.at[pl.ds(0, len(col_sends) * 16)], csend.at[0])
    for r in range(8):

        @pl.when(is_role[r])
        def _(r=r):
            for i in range(3):
                sent = sum(1 for step in PLAN if step[0] == "r" and step[1 + r] & (64 << i))
                if sent:
                    arrived(hacc.at[pl.ds(0, sent * 8)], rsend.at[i])

    arrived(yrecv.at[pl.ds(0, 7)], yrs_s.at[0])
    arrived(ypt.at[pl.ds(0, 7 * share // 2)], yag_s.at[0])
    arrived(yt.at[pl.ds(0, 15)], ywd_s.at[0])
    arrived(prodrecv.at[pl.ds(0, 7)], prs_s.at[0])
    arrived(grecv.at[pl.ds(0, 7)], grs_s.at[0])
    arrived(gpart.at[pl.ds(0, 15 * gshare)], gag_s.at[0])


def store(prod, gram, hess, out_prod, out_gram, out_h, sem):
    parts = 8
    step = hess.shape[0] // parts
    copies = [
        pltpu.make_async_copy(hess.at[pl.ds(i * step, step)], out_h.at[pl.ds(i * step, step)], sem.at[i])
        for i in range(parts)
    ]
    copies.append(pltpu.make_async_copy(prod, out_prod, sem.at[parts]))
    copies.append(pltpu.make_async_copy(gram, out_gram, sem.at[parts + 1]))
    for copy in copies:
        copy.start()
    for copy in copies:
        copy.wait()


def body(activations, weight_tile, codes, group_scales, right_factor):
    piece_tokens, feats = activations.shape
    out_rows = weight_tile.shape[0]
    rank = right_factor.shape[1]
    groups = group_scales.shape[1]
    assert piece_tokens == PIECE
    dma = pltpu.SemaphoreType.DMA
    any_spec = pl.BlockSpec(memory_space=pl.ANY)
    vmem_spec = pl.BlockSpec(memory_space=pltpu.VMEM)
    shapes = (((out_rows // 8, rank), F32), ((rank, rank), F32), ((out_rows, feats), BF16))
    parts = pl.pallas_call(
        kernel,
        out_shape=tuple(pltpu.VMEM(s, d) for s, d in shapes),
        in_specs=[any_spec] * 5,
        out_specs=(vmem_spec,) * 3,
        scratch_shapes=[
            pltpu.VMEM((16, PIECE, feats), BF16),
            pltpu.VMEM((16, PIECE, feats // 2), BF16),
            pltpu.VMEM((out_rows, feats), F32),
            pltpu.VMEM((out_rows, feats), BF16),
            pltpu.VMEM((out_rows, feats), jnp.int32),
            pltpu.VMEM((groups, out_rows), F32),
            pltpu.VMEM((out_rows, groups), F32),
            pltpu.VMEM((feats, rank), BF16),
            pltpu.VMEM((rank, PIECE), F32),
            pltpu.VMEM((8, rank // 8, PIECE), F32),
            pltpu.VMEM((16, rank, PIECE), BF16),
            pltpu.VMEM((rank, feats), BF16),
            pltpu.VMEM((out_rows, rank), BF16),
            pltpu.VMEM((8, out_rows // 8, rank), BF16),
            pltpu.VMEM((rank, rank), F32),
            pltpu.VMEM((8, rank // 16, rank), F32),
            pltpu.VMEM((rank, rank), F32),
            dma((11,)),
            dma((16, 4)),
            dma((1,)),
            dma((16, 4)),
            dma((3,)),
            dma((8,)), dma((1,)), dma((8,)), dma((1,)), dma((16, 2)), dma((1,)),
            dma((8,)), dma((1,)), dma((8,)), dma((1,)), dma((16,)), dma((1,)),
        ],
        compiler_params=pltpu.CompilerParams(
            collective_id=0, has_side_effects=True, vmem_limit_bytes=52 << 20
        ),
    )(activations, weight_tile, codes, group_scales.T, right_factor)
    return tuple(pl.pallas_call(
        store,
        out_shape=tuple(jax.ShapeDtypeStruct(s, d) for s, d in shapes),
        in_specs=[vmem_spec] * 3,
        out_specs=(any_spec,) * 3,
        scratch_shapes=[dma((10,))],
        compiler_params=pltpu.CompilerParams(vmem_limit_bytes=8 << 20),
    )(*parts))


def solution(mesh):
    spec = P("wide", "narrow")
    return jax.shard_map(
        body,
        mesh=mesh,
        in_specs=(spec, spec, spec, spec, P()),
        out_specs=(P(("wide", "narrow"), None), P(), spec),
        check_vma=False,
    )
```
